32 devices in a mesh: rep: 2 (over core), grp: 16 (over z, y, x).
Axes of the slice: x: 2, y: 2, z: 4, core: 2. Of those that a mesh axis runs over, the one named last changes fastest.
Arguments:
- grad_parts: float32 [2, 1024, 9216], P('rep', 'grp'), may hold values from -6 to 6
- gain_grad_parts: float32 [2, 2, 1024], P('rep', None, 'grp'), may hold values from -6 to 6
- weights: float32 [1024, 9216], P('grp'), may hold values from -0.1875 to 0.1875
- basis: float32 [1024, 256], P('grp'), may hold values from -0.1875 to 0.1875
- moment_first: float32 [9216, 256], P('grp'), may hold values from -12 to 12
- moment_second: float32 [9216, 256], P('grp'), may hold values from 0.01 to 1
- gains: float32 [2, 1024], P(None, 'grp'), may hold values from 0.5 to 1.5
- gain_first: float32 [2, 1024], P(None, 'grp'), may hold values from -12 to 12
- gain_second: float32 [2, 1024], P(None, 'grp'), may hold values from 0.01 to 1
Outputs:
- new_weights: float32 [1024, 9216], P('grp')
- new_first: float32 [9216, 256], P('grp')
- new_second: float32 [9216, 256], P('grp')
- new_basis: float32 [1024, 256], P('grp')
- new_gains: float32 [2, 1024], P(None, 'grp')
- new_gain_first: float32 [2, 1024], P(None, 'grp')
- new_gain_second: float32 [2, 1024], P(None, 'grp')
The draws below stay inside these ranges and needn't reach their ends.
All inputs are finite; a program needn't handle non-finite values.
Results may differ from the reference program's by a relative error of at most 0.0001.
Values sent between devices are 32-bit elements; how exact they have to be, the bound alone decides.
A program may use at most 64 MiB of HBM per device.

```python
import math
import jax
import jax.numpy as jnp
from jax import lax

D = 1024
RANK = 256
NS_STEPS = 3
NCOL = 9216
N_REP = 2


def shard_levels(own_key, shape, cuts, smallest, top_value):
    loudness, own = 1.0, jax.random.fold_in(own_key, 6)
    for axis_at, blocks in cuts:
        draws = jnp.exp(jax.random.uniform(jax.random.fold_in(own, axis_at), (blocks,), jnp.float32, smallest / len(cuts), top_value / len(cuts)))
        loudness = loudness * jnp.repeat(draws, shape[axis_at] // blocks).reshape([-1 if axis == axis_at else 1 for axis in range(len(shape))])
    return loudness


def bell_draw(rng, shape, deviation, limit, cuts=(), dtype=jnp.bfloat16):
    result = jax.random.normal(rng, shape, jnp.float32) * deviation
    if len(cuts) > 0:
        result = shard_levels(rng, shape, cuts, -0.22, 0.18) * result
    return jnp.clip(result, min=-limit, max=limit).astype(dtype)


def setup_inputs(seed: int = 0) -> dict:
    seeds = jax.random.split(jax.random.key(seed), 10)
    return {
        "grad_parts": bell_draw(seeds[0], (N_REP, D, NCOL), 1.0, 6.0, ((0, 2), (1, 16)), jnp.float32),
        "gain_grad_parts": bell_draw(seeds[1], (N_REP, 2, D), 1.0, 6.0, ((0, 2), (2, 16)), jnp.float32),
        "weights": bell_draw(seeds[2], (D, NCOL), D ** -0.5, 0.1875, ((0, 16),), jnp.float32),
        "basis": bell_draw(seeds[3], (D, RANK), D ** -0.5, 0.1875, ((0, 16),), jnp.float32),
        "moment_first": bell_draw(seeds[4], (NCOL, RANK), 2.0, 12.0, ((0, 16),), jnp.float32),
        "moment_second": jnp.clip(jnp.exp(math.log(1.0) - 4.6051702 * jax.random.uniform(seeds[5], (NCOL, RANK), jnp.float32) ** shard_levels(seeds[5], (NCOL, RANK), ((0, 16),), -0.2, 0.2)), 0.01, 1.0),
        "gains": jnp.clip(1.0 + 0.1 * jax.random.normal(seeds[6], (2, D), jnp.float32), 0.5, 1.5),
        "gain_first": bell_draw(seeds[7], (2, D), 2.0, 12.0, ((1, 16),), jnp.float32),
        "gain_second": jnp.clip(jnp.exp(math.log(1.0) - 4.6051702 * jax.random.uniform(seeds[8], (2, D), jnp.float32) ** shard_levels(seeds[8], (2, D), ((1, 16),), -0.2, 0.2)), 0.01, 1.0),
    }


beta_first = 0.9
beta_second = 0.999
learn_rate = 0.1
galore_scale = 0.25
adam_eps = 1e-08

def exact_dot(left, right):
    return jnp.dot(left, right, precision=lax.Precision.HIGHEST, preferred_element_type=jnp.float32)

def reference(grad_parts, gain_grad_parts, weights, basis, moment_first, moment_second, gains, gain_first, gain_second):
    corr_first = 1.0 - beta_first ** 10
    corr_second = 1.0 - beta_second ** 10
    grad = lax.optimization_barrier(jnp.sum(grad_parts, axis=0))
    gain_grad = lax.optimization_barrier(jnp.sum(gain_grad_parts, axis=0))
    projected = exact_dot(grad.T, basis)
    new_first = beta_first * moment_first + (1.0 - beta_first) * projected
    new_second = beta_second * moment_second + (1.0 - beta_second) * projected * projected
    direction = new_first / corr_first / (jnp.sqrt(new_second / corr_second) + adam_eps)
    new_weights = weights - learn_rate * galore_scale * exact_dot(basis, direction.T)
    subspace = exact_dot(grad, projected)
    gram = exact_dot(subspace.T, subspace)
    scale = jnp.sqrt(jnp.sqrt(jnp.sum(gram * gram) + 1e-06))
    iterate = subspace / scale
    for step in range(NS_STEPS):
        iterate = 1.5 * iterate - 0.5 * exact_dot(iterate, exact_dot(iterate.T, iterate))
    new_gain_first = beta_first * gain_first + (1.0 - beta_first) * gain_grad
    new_gain_second = beta_second * gain_second + (1.0 - beta_second) * gain_grad * gain_grad
    new_gains = gains - learn_rate * (new_gain_first / corr_first) / (jnp.sqrt(new_gain_second / corr_second) + adam_eps)
    return (new_weights, new_first, new_second, iterate, new_gains, new_gain_first, new_gain_second)
```

```python
import jax
import jax.numpy as jnp
from jax import lax
from jax.sharding import PartitionSpec as P

NS_STEPS = 3


beta_first = 0.9
beta_second = 0.999
learn_rate = 0.1
galore_scale = 0.25
adam_eps = 1e-08


def exact_dot(left, right):
    return jnp.dot(left, right, precision=lax.Precision.HIGHEST, preferred_element_type=jnp.float32)


def body(
    grad_parts,
    gain_grad_parts,
    weights,
    basis,
    moment_first,
    moment_second,
    gains,
    gain_first,
    gain_second,
):
    corr_first = 1.0 - beta_first**10
    corr_second = 1.0 - beta_second**10
    n = lax.axis_size("grp")
    rep = lax.axis_index("rep")
    swap = [(0, 1), (1, 0)]
    local_grad = grad_parts[0]
    local_gain = gain_grad_parts[0]
    rows, ncol = local_grad.shape
    half = rows // 2
    block = ncol // n
    rank = basis.shape[1]

    def own_half(x):
        return lax.dynamic_slice_in_dim(x, rep * half, half, 0)

    def other_half(x):
        return lax.dynamic_slice_in_dim(x, (1 - rep) * half, half, 0)

    def swapped(x):
        return lax.ppermute(x, "rep", swap)

    def joined(mine, other):
        return jnp.where(rep == 0, jnp.concatenate([mine, other], 0), jnp.concatenate([other, mine], 0))

    def exchange(x):
        return lax.all_to_all(x, "grp", split_axis=0, concat_axis=0, tiled=True)

    def gathered(x):
        return exchange(jnp.tile(x, (n, 1)))

    half_basis = gathered(own_half(basis))
    source = own_half(local_grad) + swapped(other_half(local_grad))
    gain_grad = local_gain + swapped(local_gain)
    col_block = lax.all_to_all(source, "grp", split_axis=1, concat_axis=0, tiled=True)
    partial = exact_dot(col_block.T, half_basis)
    projected = partial + swapped(partial)
    new_first = beta_first * moment_first + (1.0 - beta_first) * projected
    new_second = beta_second * moment_second + (1.0 - beta_second) * projected * projected
    direction = new_first / corr_first / (jnp.sqrt(new_second / corr_second) + adam_eps)
    terms = exchange(exact_dot(col_block, projected))
    sub_half = jnp.sum(terms.reshape(n, half, rank), axis=0)
    sub_all = gathered(sub_half)
    gram_half = exact_dot(sub_all.T, sub_all)
    gram = gram_half + swapped(gram_half)
    subspace = joined(sub_half, swapped(sub_half))
    update_cols = exact_dot(half_basis, direction.T)
    update = lax.all_to_all(update_cols, "grp", split_axis=0, concat_axis=1, tiled=True)
    new_half = own_half(weights) - learn_rate * galore_scale * update
    new_weights = joined(new_half, swapped(new_half))
    scale = jnp.sqrt(jnp.sqrt(jnp.sum(gram * gram) + 1e-06))
    iterate = subspace / scale
    current = gram / scale / scale
    for step in range(NS_STEPS):
        iterate = 1.5 * iterate - 0.5 * exact_dot(iterate, current)
        if step + 1 < NS_STEPS:
            side = 1.5 * current - 0.5 * exact_dot(current, current)
            current = 1.5 * side - 0.5 * exact_dot(side, current)
    new_gain_first = beta_first * gain_first + (1.0 - beta_first) * gain_grad
    new_gain_second = beta_second * gain_second + (1.0 - beta_second) * gain_grad * gain_grad
    new_gains = gains - learn_rate * (new_gain_first / corr_first) / (
        jnp.sqrt(new_gain_second / corr_second) + adam_eps
    )
    return (new_weights, new_first, new_second, iterate, new_gains, new_gain_first, new_gain_second)


def solution(mesh):
    in_specs = (
        P("rep", "grp", None),
        P("rep", None, "grp"),
        P("grp", None),
        P("grp", None),
        P("grp", None),
        P("grp", None),
        P(None, "grp"),
        P(None, "grp"),
        P(None, "grp"),
    )
    out_specs = (
        P("grp", None),
        P("grp", None),
        P("grp", None),
        P("grp", None),
        P(None, "grp"),
        P(None, "grp"),
        P(None, "grp"),
    )
    return jax.shard_map(body, mesh=mesh, in_specs=in_specs, out_specs=out_specs, check_vma=False)
```

```python
import jax
import jax.numpy as jnp
from jax import lax
from jax.experimental import pallas as pl
from jax.experimental.pallas import tpu as pltpu
from jax.sharding import PartitionSpec as P

NS_STEPS = 3


beta_first = 0.9
beta_second = 0.999
learn_rate = 0.1
galore_scale = 0.25
adam_eps = 1e-08


def exact_dot(left, right):
    return jnp.dot(left, right, precision=lax.Precision.HIGHEST, preferred_element_type=jnp.float32)


def far_first(n):
    return sorted(range(1, n), key=lambda k: abs(k - n // 2))


def peer_copy(src, dst, send_sem, recv_sem, where):
    return pltpu.make_async_remote_copy(
        src_ref=src,
        dst_ref=dst,
        send_sem=send_sem,
        recv_sem=recv_sem,
        device_id=where,
        device_id_type=pl.DeviceIdType.MESH,
    )


def greet(others):
    barrier = pltpu.get_barrier_semaphore()
    for other in others:
        pl.semaphore_signal(barrier, inc=1, device_id=other, device_id_type=pl.DeviceIdType.MESH)
    pl.semaphore_wait(barrier, len(others))


def scatter_grad(n, grad, basis, cols, full, swap, parts, swap_sems, basis_send, basis_recv, col_send, col_recv):
    me, rep = lax.axis_index("grp"), lax.axis_index("rep")
    half = swap.shape[0]
    block = cols.shape[2]
    offsets = far_first(n)
    peers = {k: {"grp": lax.rem(me + k, n)} for k in offsets}
    greet([{"rep": 1 - rep}] + [peers[k] for k in offsets])
    own = pl.ds(pl.multiple_of(rep * half, half), half)
    other = pl.ds(pl.multiple_of((1 - rep) * half, half), half)
    trade = peer_copy(grad.at[other], swap, swap_sems.at[0], swap_sems.at[1], {"rep": 1 - rep})
    trade.start()
    copies = []
    for k in offsets:
        copies.append(peer_copy(basis.at[own], full.at[me], basis_send.at[k], basis_recv.at[k], peers[k]))
        copies[-1].start()
    full[pl.ds(me, 1)] = basis[own][None]
    trade.wait()
    for j in range(n):
        parts[j] = grad[own, j * block : (j + 1) * block] + swap[:, j * block : (j + 1) * block]
    cols[pl.ds(me, 1)] = parts[pl.ds(me, 1)]
    for k in offsets:
        target = peers[k]["grp"]
        copies.append(peer_copy(parts.at[target], cols.at[me], col_send.at[k], col_recv.at[k], peers[k]))
        copies[-1].start()
    for copy in copies:
        copy.wait()


def reduce_and_return(n, terms, moved, rows, update, arrived, term_send, term_recv, row_send, row_recv, up_send, up_recv):
    me = lax.axis_index("grp")
    offsets = far_first(n)
    peers = {k: {"grp": lax.rem(me + k, n)} for k in offsets}
    greet([peers[k] for k in offsets])

    def send_update(some):
        for k in some:
            copy = peer_copy(moved.at[peers[k]["grp"]], update.at[me], up_send.at[k], up_recv.at[k], peers[k])
            copy.start()
            late.append(copy)

    late, early = [], []
    for k in offsets:
        copy = peer_copy(terms.at[peers[k]["grp"]], arrived.at[me], term_send.at[k], term_recv.at[k], peers[k])
        copy.start()
        early.append(copy)
    first = n // 4
    send_update(offsets[:first])
    arrived[pl.ds(me, 1)] = terms[pl.ds(me, 1)]
    update[pl.ds(me, 1)] = moved[pl.ds(me, 1)]
    for copy in early:
        copy.wait()
    total = arrived[0]
    for j in range(1, n):
        total = total + arrived[j]
    rows[pl.ds(me, 1)] = total[None]
    send_update(offsets[first : first + 2])
    for k in offsets:
        copy = peer_copy(rows.at[me], rows.at[me], row_send.at[k], row_recv.at[k], peers[k])
        copy.start()
        late.append(copy)
    send_update(offsets[first + 2 :])
    for copy in late:
        copy.wait()


def in_vmem(count):
    return [pl.BlockSpec(memory_space=pltpu.VMEM)] * count


def call_scatter(n, grad, basis):
    rows, ncol = grad.shape
    half, block, rank = rows // 2, ncol // n, basis.shape[1]
    sems = pltpu.SemaphoreType.DMA((n,))
    return pl.pallas_call(
        lambda *refs: scatter_grad(n, *refs),
        out_shape=(
            jax.ShapeDtypeStruct((n, half, block), jnp.float32),
            jax.ShapeDtypeStruct((n, half, rank), jnp.float32),
        ),
        in_specs=in_vmem(2),
        out_specs=tuple(in_vmem(2)),
        scratch_shapes=[
            pltpu.VMEM((half, ncol), jnp.float32),
            pltpu.VMEM((n, half, block), jnp.float32),
            pltpu.SemaphoreType.DMA((2,)),
            sems,
            sems,
            sems,
            sems,
        ],
        compiler_params=pltpu.CompilerParams(collective_id=0, has_side_effects=True),
        name="scatter_grad",
    )(grad, basis)


def call_return(n, terms, moved):
    sems = pltpu.SemaphoreType.DMA((n,))
    return pl.pallas_call(
        lambda *refs: reduce_and_return(n, *refs),
        out_shape=(
            jax.ShapeDtypeStruct(terms.shape, jnp.float32),
            jax.ShapeDtypeStruct(moved.shape, jnp.float32),
        ),
        in_specs=in_vmem(2),
        out_specs=tuple(in_vmem(2)),
        scratch_shapes=[pltpu.VMEM(terms.shape, jnp.float32)] + [sems] * 6,
        compiler_params=pltpu.CompilerParams(collective_id=1, has_side_effects=True),
        name="reduce_and_return",
    )(terms, moved)


def body(
    grad_parts,
    gain_grad_parts,
    weights,
    basis,
    moment_first,
    moment_second,
    gains,
    gain_first,
    gain_second,
):
    corr_first = 1.0 - beta_first**10
    corr_second = 1.0 - beta_second**10
    n = lax.axis_size("grp")
    rep = lax.axis_index("rep")
    swap = [(0, 1), (1, 0)]
    local_grad = grad_parts[0]
    local_gain = gain_grad_parts[0]
    rows, ncol = local_grad.shape
    half = rows // 2
    block = ncol // n
    rank = basis.shape[1]

    def own_half(x):
        return lax.dynamic_slice_in_dim(x, rep * half, half, 0)

    def swapped(x):
        return lax.ppermute(x, "rep", swap)

    def joined(mine, other):
        return jnp.where(rep == 0, jnp.concatenate([mine, other], 0), jnp.concatenate([other, mine], 0))

    gain_grad = local_gain + swapped(local_gain)
    col_block, half_basis = call_scatter(n, local_grad, basis)
    col_block = col_block.reshape(n * half, block)
    half_basis = half_basis.reshape(n * half, rank)
    partial = exact_dot(col_block.T, half_basis)
    projected = partial + swapped(partial)
    new_first = beta_first * moment_first + (1.0 - beta_first) * projected
    new_second = beta_second * moment_second + (1.0 - beta_second) * projected * projected
    direction = new_first / corr_first / (jnp.sqrt(new_second / corr_second) + adam_eps)
    terms = exact_dot(col_block, projected).reshape(n, half, rank)
    update_cols = exact_dot(half_basis, direction.T).reshape(n, half, block)
    sub_all, update = call_return(n, terms, update_cols)
    sub_half = lax.dynamic_index_in_dim(sub_all, lax.axis_index("grp"), 0, keepdims=False)
    sub_all = sub_all.reshape(n * half, rank)
    update = jnp.swapaxes(update, 0, 1).reshape(half, ncol)
    gram_half = exact_dot(sub_all.T, sub_all)
    gram = gram_half + swapped(gram_half)
    subspace = joined(sub_half, swapped(sub_half))
    new_half = own_half(weights) - learn_rate * galore_scale * update
    new_weights = joined(new_half, swapped(new_half))
    scale = jnp.sqrt(jnp.sqrt(jnp.sum(gram * gram) + 1e-06))
    iterate = subspace / scale
    current = gram / scale / scale
    for step in range(NS_STEPS):
        iterate = 1.5 * iterate - 0.5 * exact_dot(iterate, current)
        if step + 1 < NS_STEPS:
            side = 1.5 * current - 0.5 * exact_dot(current, current)
            current = 1.5 * side - 0.5 * exact_dot(side, current)
    new_gain_first = beta_first * gain_first + (1.0 - beta_first) * gain_grad
    new_gain_second = beta_second * gain_second + (1.0 - beta_second) * gain_grad * gain_grad
    new_gains = gains - learn_rate * (new_gain_first / corr_first) / (
        jnp.sqrt(new_gain_second / corr_second) + adam_eps
    )
    return (new_weights, new_first, new_second, iterate, new_gains, new_gain_first, new_gain_second)


def solution(mesh):
    in_specs = (
        P("rep", "grp", None),
        P("rep", None, "grp"),
        P("grp", None),
        P("grp", None),
        P("grp", None),
        P("grp", None),
        P(None, "grp"),
        P(None, "grp"),
        P(None, "grp"),
    )
    out_specs = (
        P("grp", None),
        P("grp", None),
        P("grp", None),
        P("grp", None),
        P(None, "grp"),
        P(None, "grp"),
        P(None, "grp"),
    )
    return jax.shard_map(body, mesh=mesh, in_specs=in_specs, out_specs=out_specs, check_vma=False)
```

```python
import jax
import jax.numpy as jnp
from jax import lax
from jax.experimental import pallas as pl
from jax.experimental.pallas import tpu as pltpu
from jax.sharding import PartitionSpec as P

NS_STEPS = 3
GRANT = 24 << 20


beta_first = 0.9
beta_second = 0.999
learn_rate = 0.1
galore_scale = 0.25
adam_eps = 1e-08


def exact_dot(left, right):
    return jnp.dot(left, right, precision=lax.Precision.HIGHEST, preferred_element_type=jnp.float32)


def far_first(n):
    return sorted(range(1, n), key=lambda k: abs(k - n // 2))


def peer_copy(src, dst, send_sem, recv_sem, where):
    return pltpu.make_async_remote_copy(
        src_ref=src,
        dst_ref=dst,
        send_sem=send_sem,
        recv_sem=recv_sem,
        device_id=where,
        device_id_type=pl.DeviceIdType.MESH,
    )


def greet(others):
    barrier = pltpu.get_barrier_semaphore()
    for other in others:
        pl.semaphore_signal(barrier, inc=1, device_id=other, device_id_type=pl.DeviceIdType.MESH)
    pl.semaphore_wait(barrier, len(others))


def groups(n):
    fan = 4 if n % 4 == 0 else 1
    return n // fan, fan


def peer_maps(n, me):
    depth, fan = groups(n)
    layer, spot = me // fan, lax.rem(me, fan)
    column = {d: lax.rem(layer + d, depth) * fan + spot for d in range(1, depth)}
    plane = {f: layer * fan + lax.rem(spot + f, fan) for f in range(1, fan)}
    return layer, spot, column, plane


def spread(n, me, ref, send, recv, sent):
    depth, fan = groups(n)
    layer, spot, column, plane = peer_maps(n, me)
    down = []
    for d in sorted(column, key=lambda d: abs(d - depth // 2)):
        down.append((d, peer_copy(ref.at[me], ref.at[me], send.at[d * fan], recv.at[d * fan], {"grp": column[d]})))
        down[-1][1].start()
    for f in plane:
        sent.append(peer_copy(ref.at[me], ref.at[me], send.at[f], recv.at[f], {"grp": plane[f]}))
        sent[-1].start()

    def pass_on():
        for d, copy in down:
            copy.wait()
            slot = lax.rem(layer - d + depth, depth) * fan + spot
            for f in plane:
                at = d * fan + f
                sent.append(peer_copy(ref.at[slot], ref.at[slot], send.at[at], recv.at[at], {"grp": plane[f]}))
                sent[-1].start()

    return pass_on


def scatter_grad(n, grad, basis, cols, full, swap, parts, swap_sems, basis_send, basis_recv, col_send, col_recv):
    me, rep = lax.axis_index("grp"), lax.axis_index("rep")
    half = swap.shape[0]
    block = cols.shape[2]
    offsets = far_first(n)
    peers = {k: {"grp": lax.rem(me + k, n)} for k in offsets}
    own = pl.ds(pl.multiple_of(rep * half, half), half)
    other = pl.ds(pl.multiple_of((1 - rep) * half, half), half)
    full[pl.ds(me, 1)] = basis[own][None]
    greet([{"rep": 1 - rep}] + [peers[k] for k in offsets])
    trade = peer_copy(grad.at[other], swap, swap_sems.at[0], swap_sems.at[1], {"rep": 1 - rep})
    trade.start()
    copies = []
    pass_on = spread(n, me, full, basis_send, basis_recv, copies)
    trade.wait()
    for j in range(n):
        parts[j] = grad[own, j * block : (j + 1) * block] + swap[:, j * block : (j + 1) * block]
    cols[pl.ds(me, 1)] = parts[pl.ds(me, 1)]
    late = n // 4
    for at, k in enumerate(offsets):
        if at == late:
            pass_on()
        target = peers[k]["grp"]
        copies.append(peer_copy(parts.at[target], cols.at[me], col_send.at[k], col_recv.at[k], peers[k]))
        copies[-1].start()
    for copy in copies:
        copy.wait()


def reduce_and_return(
    n, terms, moved, rows, update, near, sums, far, near_send, near_recv, far_send, far_recv, row_send, row_recv, up_send, up_recv
):
    me = lax.axis_index("grp")
    depth, fan = groups(n)
    layer, spot, column, plane = peer_maps(n, me)
    offsets = far_first(n)
    peers = {k: {"grp": lax.rem(me + k, n)} for k in offsets}
    greet([peers[k] for k in offsets])
    late = []
    waiting = list(offsets)

    def send_update(count):
        for k in waiting[:count]:
            copy = peer_copy(moved.at[peers[k]["grp"]], update.at[me], up_send.at[k], up_recv.at[k], peers[k])
            copy.start()
            late.append(copy)
        del waiting[:count]

    first = []
    for f in plane:
        source = terms.at[:, lax.rem(spot + f, fan)]
        first.append(peer_copy(source, near.at[f], near_send.at[f], near_recv.at[f], {"grp": plane[f]}))
        first[-1].start()
    send_update(n // 4)
    update[pl.ds(me, 1)] = moved[pl.ds(me, 1)]
    near[0] = terms[:, pl.ds(spot, 1)][:, 0]
    for copy in first:
        copy.wait()
    partial = near[0]
    for f in plane:
        partial = partial + near[f]
    sums[...] = partial
    second = []
    for d in column:
        source = sums.at[lax.rem(layer + d, depth)]
        second.append(peer_copy(source, far.at[d], far_send.at[d], far_recv.at[d], {"grp": column[d]}))
        second[-1].start()
    send_update(n // 8)
    far[0] = sums[pl.ds(layer, 1)][0]
    for copy in second:
        copy.wait()
    total = far[0]
    for d in column:
        total = total + far[d]
    rows[pl.ds(me, 1)] = total[None]
    pass_on = spread(n, me, rows, row_send, row_recv, late)
    send_update(n // 4)
    pass_on()
    send_update(n)
    for copy in late:
        copy.wait()


def in_vmem(count):
    return [pl.BlockSpec(memory_space=pltpu.VMEM)] * count


def call_scatter(n, grad, basis):
    rows, ncol = grad.shape
    half, block, rank = rows // 2, ncol // n, basis.shape[1]
    sems = pltpu.SemaphoreType.DMA((n,))
    return pl.pallas_call(
        lambda *refs: scatter_grad(n, *refs),
        out_shape=(
            jax.ShapeDtypeStruct((n, half, block), jnp.float32),
            jax.ShapeDtypeStruct((n, half, rank), jnp.float32),
        ),
        in_specs=in_vmem(2),
        out_specs=tuple(in_vmem(2)),
        scratch_shapes=[
            pltpu.VMEM((half, ncol), jnp.float32),
            pltpu.VMEM((n, half, block), jnp.float32),
            pltpu.SemaphoreType.DMA((2,)),
            sems,
            sems,
            sems,
            sems,
        ],
        compiler_params=pltpu.CompilerParams(collective_id=0, has_side_effects=True, vmem_limit_bytes=GRANT),
        name="scatter_grad",
    )(grad, basis)


def call_return(n, terms, moved):
    half, rank = terms.shape[2:]
    depth, fan = groups(n)
    sems = pltpu.SemaphoreType.DMA((n,))
    return pl.pallas_call(
        lambda *refs: reduce_and_return(n, *refs),
        out_shape=(
            jax.ShapeDtypeStruct((n, half, rank), jnp.float32),
            jax.ShapeDtypeStruct(moved.shape, jnp.float32),
        ),
        in_specs=in_vmem(2),
        out_specs=tuple(in_vmem(2)),
        scratch_shapes=[
            pltpu.VMEM((fan, depth, half, rank), jnp.float32),
            pltpu.VMEM((depth, half, rank), jnp.float32),
            pltpu.VMEM((depth, half, rank), jnp.float32),
        ]
        + [sems] * 8,
        compiler_params=pltpu.CompilerParams(collective_id=1, has_side_effects=True, vmem_limit_bytes=GRANT),
        name="reduce_and_return",
    )(terms, moved)


def body(
    grad_parts,
    gain_grad_parts,
    weights,
    basis,
    moment_first,
    moment_second,
    gains,
    gain_first,
    gain_second,
):
    corr_first = 1.0 - beta_first**10
    corr_second = 1.0 - beta_second**10
    n = lax.axis_size("grp")
    rep = lax.axis_index("rep")
    swap = [(0, 1), (1, 0)]
    local_grad = grad_parts[0]
    local_gain = gain_grad_parts[0]
    rows, ncol = local_grad.shape
    half = rows // 2
    block = ncol // n
    rank = basis.shape[1]

    def own_half(x):
        return lax.dynamic_slice_in_dim(x, rep * half, half, 0)

    def swapped(x):
        return lax.ppermute(x, "rep", swap)

    def joined(mine, other):
        return jnp.where(rep == 0, jnp.concatenate([mine, other], 0), jnp.concatenate([other, mine], 0))

    gain_grad = local_gain + swapped(local_gain)
    col_block, half_basis = call_scatter(n, local_grad, basis)
    col_block = col_block.reshape(n * half, block)
    half_basis = half_basis.reshape(n * half, rank)
    partial = exact_dot(col_block.T, half_basis)
    projected = partial + swapped(partial)
    new_first = beta_first * moment_first + (1.0 - beta_first) * projected
    new_second = beta_second * moment_second + (1.0 - beta_second) * projected * projected
    direction = new_first / corr_first / (jnp.sqrt(new_second / corr_second) + adam_eps)
    terms = exact_dot(col_block, projected).reshape(*groups(n), half, rank)
    update_cols = exact_dot(half_basis, direction.T).reshape(n, half, block)
    sub_all, update = call_return(n, terms, update_cols)
    sub_half = lax.dynamic_index_in_dim(sub_all, lax.axis_index("grp"), 0, keepdims=False)
    sub_all = sub_all.reshape(n * half, rank)
    update = jnp.swapaxes(update, 0, 1).reshape(half, ncol)
    gram_half = exact_dot(sub_all.T, sub_all)
    gram = gram_half + swapped(gram_half)
    subspace = joined(sub_half, swapped(sub_half))
    new_half = own_half(weights) - learn_rate * galore_scale * update
    new_weights = joined(new_half, swapped(new_half))
    scale = jnp.sqrt(jnp.sqrt(jnp.sum(gram * gram) + 1e-06))
    iterate = subspace / scale
    current = gram / scale / scale
    for step in range(NS_STEPS):
        iterate = 1.5 * iterate - 0.5 * exact_dot(iterate, current)
        if step + 1 < NS_STEPS:
            side = 1.5 * current - 0.5 * exact_dot(current, current)
            current = 1.5 * side - 0.5 * exact_dot(side, current)
    new_gain_first = beta_first * gain_first + (1.0 - beta_first) * gain_grad
    new_gain_second = beta_second * gain_second + (1.0 - beta_second) * gain_grad * gain_grad
    new_gains = gains - learn_rate * (new_gain_first / corr_first) / (
        jnp.sqrt(new_gain_second / corr_second) + adam_eps
    )
    return (new_weights, new_first, new_second, iterate, new_gains, new_gain_first, new_gain_second)


def solution(mesh):
    in_specs = (
        P("rep", "grp", None),
        P("rep", None, "grp"),
        P("grp", None),
        P("grp", None),
        P("grp", None),
        P("grp", None),
        P(None, "grp"),
        P(None, "grp"),
        P(None, "grp"),
    )
    out_specs = (
        P("grp", None),
        P("grp", None),
        P("grp", None),
        P("grp", None),
        P(None, "grp"),
        P(None, "grp"),
        P(None, "grp"),
    )
    return jax.shard_map(body, mesh=mesh, in_specs=in_specs, out_specs=out_specs, check_vma=False)
```

```python
import jax
import jax.numpy as jnp
from jax import lax
from jax.experimental import pallas as pl
from jax.experimental.pallas import tpu as pltpu
from jax.sharding import PartitionSpec as P

NS_STEPS = 3
GRANT = 24 << 20


beta_first = 0.9
beta_second = 0.999
learn_rate = 0.1
galore_scale = 0.25
adam_eps = 1e-08


def exact_dot(left, right):
    return jnp.dot(left, right, precision=lax.Precision.HIGHEST, preferred_element_type=jnp.float32)


def far_first(n):
    return sorted(range(1, n), key=lambda k: abs(k - n // 2))


def peer_copy(src, dst, send_sem, recv_sem, where):
    return pltpu.make_async_remote_copy(
        src_ref=src,
        dst_ref=dst,
        send_sem=send_sem,
        recv_sem=recv_sem,
        device_id=where,
        device_id_type=pl.DeviceIdType.MESH,
    )


def greet(others):
    barrier = pltpu.get_barrier_semaphore()
    for other in others:
        pl.semaphore_signal(barrier, inc=1, device_id=other, device_id_type=pl.DeviceIdType.MESH)
    pl.semaphore_wait(barrier, len(others))


def groups(n):
    fan = 4 if n % 4 == 0 else 1
    return n // fan, fan


def peer_maps(n, me):
    depth, fan = groups(n)
    layer, spot = me // fan, lax.rem(me, fan)
    column = {d: lax.rem(layer + d, depth) * fan + spot for d in range(1, depth)}
    plane = {f: layer * fan + lax.rem(spot + f, fan) for f in range(1, fan)}
    return layer, spot, column, plane


def spread(n, me, ref, send, recv, sent):
    depth, fan = groups(n)
    layer, spot, column, plane = peer_maps(n, me)
    down = []
    for d in sorted(column, key=lambda d: abs(d - depth // 2)):
        down.append((d, peer_copy(ref.at[me], ref.at[me], send.at[d * fan], recv.at[d * fan], {"grp": column[d]})))
        down[-1][1].start()
    for f in plane:
        sent.append(peer_copy(ref.at[me], ref.at[me], send.at[f], recv.at[f], {"grp": plane[f]}))
        sent[-1].start()

    def pass_on():
        for d, copy in down:
            copy.wait()
            slot = lax.rem(layer - d + depth, depth) * fan + spot
            for f in plane:
                at = d * fan + f
                sent.append(peer_copy(ref.at[slot], ref.at[slot], send.at[at], recv.at[at], {"grp": plane[f]}))
                sent[-1].start()

    return pass_on


def split_of(half, block):
    rest = block % 128
    return (block - rest, rest) if 2 * rest == 128 and half % 16 == 0 else (block, 0)


def tails_of(n, half, block):
    rest = split_of(half, block)[1]
    return pltpu.VMEM((n, half // 2, 128) if rest else (1, 8, 128), jnp.float32)


def pack_tails(ref, tails):
    half = ref.shape[1]
    main, rest = split_of(half, ref.shape[2])
    if rest:
        tails[:, :, :rest] = ref[:, : half // 2, main:]
        tails[:, :, rest:] = ref[:, half // 2 :, main:]


def unpack_tails(tails, ref):
    half = ref.shape[1]
    main, rest = split_of(half, ref.shape[2])
    if rest:
        ref[:, : half // 2, main:] = tails[:, :, :rest]
        ref[:, half // 2 :, main:] = tails[:, :, rest:]


def keep_own(me, source, target, tails_out, tails_in):
    target[pl.ds(me, 1)] = source[pl.ds(me, 1)]
    if split_of(*source.shape[1:])[1]:
        tails_in[pl.ds(me, 1)] = tails_out[pl.ds(me, 1)]


def send_block(me, k, where, source, target, tails_out, tails_in, send, recv):
    main, rest = split_of(*source.shape[1:])
    peer = where["grp"]
    copies = [peer_copy(source.at[peer, :, :main], target.at[me, :, :main], send.at[0, k], recv.at[0, k], where)]
    if rest:
        copies.append(peer_copy(tails_out.at[peer], tails_in.at[me], send.at[1, k], recv.at[1, k], where))
    for copy in copies:
        copy.start()
    return copies


def scatter_grad(n, grad, basis, cols, full, mine, swap, parts, tails_out, tails_in, load_sem, swap_sems, basis_send, basis_recv, col_send, col_recv):
    me, rep = lax.axis_index("grp"), lax.axis_index("rep")
    half = swap.shape[0]
    block = cols.shape[2]
    offsets = far_first(n)
    peers = {k: {"grp": lax.rem(me + k, n)} for k in offsets}
    own = pl.ds(pl.multiple_of(rep * half, half), half)
    other = pl.ds(pl.multiple_of((1 - rep) * half, half), half)
    load = pltpu.make_async_copy(grad.at[own], mine, load_sem)
    load.start()
    full[pl.ds(me, 1)] = basis[own][None]
    greet([{"rep": 1 - rep}] + [peers[k] for k in offsets])
    trade = peer_copy(grad.at[other], swap, swap_sems.at[0], swap_sems.at[1], {"rep": 1 - rep})
    trade.start()
    copies = []
    pass_on = spread(n, me, full, basis_send, basis_recv, copies)
    load.wait()
    trade.wait()
    for j in range(n):
        parts[j] = mine[:, j * block : (j + 1) * block] + swap[:, j * block : (j + 1) * block]
    pack_tails(parts, tails_out)
    keep_own(me, parts, cols, tails_out, tails_in)
    late = n // 4
    for at, k in enumerate(offsets):
        if at == late:
            pass_on()
        copies += send_block(me, k, peers[k], parts, cols, tails_out, tails_in, col_send, col_recv)
    for copy in copies:
        copy.wait()
    unpack_tails(tails_in, cols)


def reduce_and_return(
    n, terms, moved, rows, update, near, sums, far, tails_out, tails_in, near_send, near_recv, far_send, far_recv, row_send, row_recv, up_send, up_recv
):
    me = lax.axis_index("grp")
    depth, fan = groups(n)
    layer, spot, column, plane = peer_maps(n, me)
    offsets = far_first(n)
    peers = {k: {"grp": lax.rem(me + k, n)} for k in offsets}
    greet([peers[k] for k in offsets])
    late = []
    waiting = list(offsets)

    def send_update(count):
        for k in waiting[:count]:
            late.extend(send_block(me, k, peers[k], moved, update, tails_out, tails_in, up_send, up_recv))
        del waiting[:count]

    first = []
    for f in plane:
        source = terms.at[:, lax.rem(spot + f, fan)]
        first.append(peer_copy(source, near.at[f], near_send.at[f], near_recv.at[f], {"grp": plane[f]}))
        first[-1].start()
    pack_tails(moved, tails_out)
    send_update(n // 4)
    keep_own(me, moved, update, tails_out, tails_in)
    near[0] = terms[:, pl.ds(spot, 1)][:, 0]
    for copy in first:
        copy.wait()
    partial = near[0]
    for f in plane:
        partial = partial + near[f]
    sums[...] = partial
    second = []
    for d in column:
        source = sums.at[lax.rem(layer + d, depth)]
        second.append(peer_copy(source, far.at[d], far_send.at[d], far_recv.at[d], {"grp": column[d]}))
        second[-1].start()
    send_update(n // 8)
    far[0] = sums[pl.ds(layer, 1)][0]
    for copy in second:
        copy.wait()
    total = far[0]
    for d in column:
        total = total + far[d]
    rows[pl.ds(me, 1)] = total[None]
    pass_on = spread(n, me, rows, row_send, row_recv, late)
    send_update(n // 4)
    pass_on()
    send_update(n)
    for copy in late:
        copy.wait()
    unpack_tails(tails_in, update)


def in_vmem(count):
    return [pl.BlockSpec(memory_space=pltpu.VMEM)] * count


def call_scatter(n, grad, basis):
    rows, ncol = grad.shape
    half, block, rank = rows // 2, ncol // n, basis.shape[1]
    sems = pltpu.SemaphoreType.DMA((n,))
    return pl.pallas_call(
        lambda *refs: scatter_grad(n, *refs),
        out_shape=(
            jax.ShapeDtypeStruct((n, half, block), jnp.float32),
            jax.ShapeDtypeStruct((n, half, rank), jnp.float32),
        ),
        in_specs=[pl.BlockSpec(memory_space=pltpu.HBM)] + in_vmem(1),
        out_specs=tuple(in_vmem(2)),
        scratch_shapes=[
            pltpu.VMEM((half, ncol), jnp.float32),
            pltpu.VMEM((half, ncol), jnp.float32),
            pltpu.VMEM((n, half, block), jnp.float32),
            tails_of(n, half, block),
            tails_of(n, half, block),
            pltpu.SemaphoreType.DMA,
            pltpu.SemaphoreType.DMA((2,)),
            sems,
            sems,
            pltpu.SemaphoreType.DMA((2, n)),
            pltpu.SemaphoreType.DMA((2, n)),
        ],
        compiler_params=pltpu.CompilerParams(collective_id=0, has_side_effects=True, vmem_limit_bytes=GRANT),
        name="scatter_grad",
    )(grad, basis)


def call_return(n, terms, moved):
    half, rank = terms.shape[2:]
    depth, fan = groups(n)
    sems = pltpu.SemaphoreType.DMA((n,))
    return pl.pallas_call(
        lambda *refs: reduce_and_return(n, *refs),
        out_shape=(
            jax.ShapeDtypeStruct((n, half, rank), jnp.float32),
            jax.ShapeDtypeStruct(moved.shape, jnp.float32),
        ),
        in_specs=in_vmem(2),
        out_specs=tuple(in_vmem(2)),
        scratch_shapes=[
            pltpu.VMEM((fan, depth, half, rank), jnp.float32),
            pltpu.VMEM((depth, half, rank), jnp.float32),
            pltpu.VMEM((depth, half, rank), jnp.float32),
            tails_of(*moved.shape),
            tails_of(*moved.shape),
        ]
        + [sems] * 6
        + [pltpu.SemaphoreType.DMA((2, n))] * 2,
        compiler_params=pltpu.CompilerParams(collective_id=1, has_side_effects=True, vmem_limit_bytes=GRANT),
        name="reduce_and_return",
    )(terms, moved)


def body(
    grad_parts,
    gain_grad_parts,
    weights,
    basis,
    moment_first,
    moment_second,
    gains,
    gain_first,
    gain_second,
):
    corr_first = 1.0 - beta_first**10
    corr_second = 1.0 - beta_second**10
    n = lax.axis_size("grp")
    rep = lax.axis_index("rep")
    swap = [(0, 1), (1, 0)]
    local_grad = grad_parts[0]
    local_gain = gain_grad_parts[0]
    rows, ncol = local_grad.shape
    half = rows // 2
    block = ncol // n
    rank = basis.shape[1]

    def own_half(x):
        return lax.dynamic_slice_in_dim(x, rep * half, half, 0)

    def swapped(x):
        return lax.ppermute(x, "rep", swap)

    def joined(mine, other):
        return jnp.where(rep == 0, jnp.concatenate([mine, other], 0), jnp.concatenate([other, mine], 0))

    gain_grad = local_gain + swapped(local_gain)
    col_block, half_basis = call_scatter(n, local_grad, basis)
    col_block = col_block.reshape(n * half, block)
    half_basis = half_basis.reshape(n * half, rank)
    partial = exact_dot(col_block.T, half_basis)
    projected = partial + swapped(partial)
    new_first = beta_first * moment_first + (1.0 - beta_first) * projected
    new_second = beta_second * moment_second + (1.0 - beta_second) * projected * projected
    direction = new_first / corr_first / (jnp.sqrt(new_second / corr_second) + adam_eps)
    terms = exact_dot(col_block, projected).reshape(*groups(n), half, rank)
    update_cols = exact_dot(half_basis, direction.T).reshape(n, half, block)
    sub_all, update = call_return(n, terms, update_cols)
    sub_half = lax.dynamic_index_in_dim(sub_all, lax.axis_index("grp"), 0, keepdims=False)
    sub_all = sub_all.reshape(n * half, rank)
    update = jnp.swapaxes(update, 0, 1).reshape(half, ncol)
    gram_half = exact_dot(sub_all.T, sub_all)
    gram = gram_half + swapped(gram_half)
    subspace = joined(sub_half, swapped(sub_half))
    new_half = own_half(weights) - learn_rate * galore_scale * update
    new_weights = joined(new_half, swapped(new_half))
    scale = jnp.sqrt(jnp.sqrt(jnp.sum(gram * gram) + 1e-06))
    iterate = subspace / scale
    current = gram / scale / scale
    for step in range(NS_STEPS):
        iterate = 1.5 * iterate - 0.5 * exact_dot(iterate, current)
        if step + 1 < NS_STEPS:
            side = 1.5 * current - 0.5 * exact_dot(current, current)
            current = 1.5 * side - 0.5 * exact_dot(side, current)
    new_gain_first = beta_first * gain_first + (1.0 - beta_first) * gain_grad
    new_gain_second = beta_second * gain_second + (1.0 - beta_second) * gain_grad * gain_grad
    new_gains = gains - learn_rate * (new_gain_first / corr_first) / (
        jnp.sqrt(new_gain_second / corr_second) + adam_eps
    )
    return (new_weights, new_first, new_second, iterate, new_gains, new_gain_first, new_gain_second)


def solution(mesh):
    in_specs = (
        P("rep", "grp", None),
        P("rep", None, "grp"),
        P("grp", None),
        P("grp", None),
        P("grp", None),
        P("grp", None),
        P(None, "grp"),
        P(None, "grp"),
        P(None, "grp"),
    )
    out_specs = (
        P("grp", None),
        P("grp", None),
        P("grp", None),
        P("grp", None),
        P(None, "grp"),
        P(None, "grp"),
        P(None, "grp"),
    )
    return jax.shard_map(body, mesh=mesh, in_specs=in_specs, out_specs=out_specs, check_vma=False)
```
